256 devices in a mesh: row: 8 (over z), col: 16 (over x_hi, y, core), rep: 2 (over x_lo).
Axes of the slice: x: 4 (x_hi: 2, x_lo: 2; x = x_hi * 2 + x_lo), y: 4, z: 8, core: 2. Of those that a mesh axis runs over, the one named last changes fastest.
Arguments:
- spectra: bfloat16 [2, 16, 64, 8192], P(None, 'row', 'rep', 'col'), parts along dimension 2, may hold values from -60 to 60, as said below
Outputs:
- correlation: bfloat16 [12, 8192, 8192], P('rep', 'row', 'col'), parts along dimension 0
The draws below stay inside these ranges and needn't reach their ends.
There are 2 independent parts, one for each index of `rep`. The reference program is written for one: setup_inputs(seed, part) draws one part's arguments, and reference() takes and returns one part's arrays. A program takes and returns all parts, laid end to end along the dimension named above; each array names one. Nothing has to cross between parts.
Inputs may be any that keep to these rules, and one draw needn't show every extreme that they name: `spectra`: spectral samples.
All inputs are finite; a program needn't handle non-finite values.
Results may differ from the reference program's by a relative error of at most 0.0065.
Values may be sent and summed in bfloat16 or wider, within the bound.
No kernel may reach another device: no remote copies, remote signals or barrier semaphores. Data moves between devices by JAX's collectives and lax.ppermute only.
A program may use at most 64 MiB of HBM per device.

```python
import math
import jax
import jax.numpy as jnp
from jax import lax

BINS = 32
LAGS = 6
CHANNELS = 8192
WINDOWS = 16


def draw_spectra(key, part):
    k_base, k_bins, k_chan = jax.random.split(key, 3)
    shape = (2, WINDOWS, BINS, CHANNELS)
    bin_scale = jnp.exp(jax.random.uniform(k_bins, (1, WINDOWS, BINS, CHANNELS), jnp.float32, math.log(0.3), math.log(3.0)))
    chan_scale = jnp.exp(jax.random.uniform(k_chan, (1, WINDOWS, 1, CHANNELS), jnp.float32, math.log(0.2), math.log(5.0)))
    base = jnp.clip(jax.random.normal(k_base, shape, jnp.float32), -4.0, 4.0)
    return (base * bin_scale * chan_scale).astype(jnp.bfloat16)


def setup_inputs(seed: int = 0, part: int = 0) -> dict:
    streams_of = jax.random.split(jax.random.key(seed), 2)
    part_keys = jax.random.split(jax.random.fold_in(streams_of[1], part), 2)
    spectra = draw_spectra(jax.random.fold_in(jax.random.fold_in(streams_of[1], part), 71), part)
    return {"spectra": spectra}


def whiten(spectra):
    values = spectra.astype(jnp.float32)
    power = lax.optimization_barrier(jnp.mean(values * values, axis=(0, 2), keepdims=True))
    return (values / jnp.sqrt(power + 1e-05)).astype(jnp.bfloat16)

def phase_tables(bins, lags):
    freq = jnp.arange(bins).astype(jnp.float32) + 1.0
    shift = 2.0 * jnp.arange(lags).astype(jnp.float32) - lags + 1.0
    angle = math.pi * shift[:, None] * freq[None, :] / bins
    return (jnp.cos(angle), jnp.sin(angle))

def reference(spectra):
    white = whiten(spectra)
    cosine, sine = phase_tables(BINS, LAGS)
    flat = white.reshape(2 * WINDOWS * BINS, CHANNELS)
    values = white.astype(jnp.float32)
    scale = 1.0 / math.sqrt(WINDOWS * BINS)

    def one_lag(tables):
        cos_row, sin_row = tables
        c_term = cos_row[None, :, None]
        s_term = sin_row[None, :, None]
        real_part = values[0] * c_term - values[1] * s_term
        imag_part = values[0] * s_term + values[1] * c_term
        turned = jnp.stack([real_part, imag_part]).astype(jnp.bfloat16).reshape(2 * WINDOWS * BINS, CHANNELS)
        summed = jnp.dot(flat.T, turned, preferred_element_type=jnp.float32)
        return (summed * scale).astype(jnp.bfloat16)
    return lax.map(one_lag, (cosine, sine))
```

```python
import functools
import math

import jax
import jax.numpy as jnp
import numpy as np
from jax import lax
from jax.experimental import pallas as pl
from jax.experimental.pallas import tpu as pltpu
from jax.sharding import PartitionSpec as P

LAGS = 6
ROWS = 8
CHIPS = 8
VMEM = pl.BlockSpec(memory_space=pltpu.VMEM)
SMEM = pl.BlockSpec(memory_space=pltpu.SMEM)
F32, BF16 = jnp.float32, jnp.bfloat16

OFFSETS = {4: (0, 0), 3: (0, 1), 5: (0, 3), 2: (1, 0), 6: (0, 2), 1: (1, 1), 7: (1, 3), 0: (1, 2)}
PLANE = ((1, 2), (1, 1), (1, 3), (1, 0), (0, 2), (0, 1), (0, 3))


def moved(chip, dx, dy):
    return ((chip // 4) ^ dx) * 4 + (chip % 4 + dy) % 4


def chip_of(z, m):
    return moved(m, *OFFSETS[(z - m) % 8])


def slot_table():
    held = np.zeros((ROWS, CHIPS), np.int32)
    for m in range(ROWS):
        for z in range(ROWS):
            held[m, chip_of(z, m)] = z
    table = np.zeros((ROWS, CHIPS, 8), np.int32)
    for m in range(ROWS):
        for chip in range(CHIPS):
            sources = [chip] + [moved(chip, dx, -dy) for dx, dy in PLANE]
            table[m, chip] = [held[m, s] for s in sources]
    return table


def transpose_rows(x):
    perm = [
        (z * 16 + m * 2 + c, m * 16 + chip_of(z, m) * 2 + c)
        for z in range(ROWS)
        for m in range(CHIPS)
        for c in range(2)
    ]
    return lax.ppermute(x, ("row", "col"), perm)


def along_z(x, step):
    return lax.ppermute(x, "row", [(i, (i + step) % ROWS) for i in range(ROWS)])


def in_plane(x, dx, dy):
    return lax.ppermute(x, "col", [(k * 2 + c, moved(k, dx, dy) * 2 + c) for k in range(CHIPS) for c in range(2)])


def other_core(x):
    return lax.ppermute(x, "col", [(j, j ^ 1) for j in range(16)])


def whiten_kernel(x_ref, white_ref, turned_ref):
    def window(w, _):
        v = x_ref[:, w].astype(F32)
        power = jnp.mean(v * v, axis=(0, 1), keepdims=True)
        white = v / jnp.sqrt(power + 1e-05)
        white_ref[:, w] = white.astype(BF16)
        return _

    for w in range(x_ref.shape[1]):
        window(w, 0)
    flat = white_ref[...].reshape(-1, x_ref.shape[3]).astype(F32)
    turned_ref[...] = flat.T.astype(BF16)


def whiten(x):
    _, w, f, n = x.shape
    return pl.pallas_call(
        whiten_kernel,
        out_shape=(jax.ShapeDtypeStruct(x.shape, BF16), jax.ShapeDtypeStruct((n, 2 * w * f), BF16)),
        in_specs=[VMEM],
        out_specs=[VMEM, VMEM],
        compiler_params=pltpu.CompilerParams(vmem_limit_bytes=8 << 20),
        name="whiten",
    )(x)


def rotate_kernel(z_ref, cos_ref, sin_ref, *refs):
    out_ref = refs[-1]
    blocks = refs[:-1]

    def turn(re_of, im_of, z, w, lanes):
        re, im = re_of.astype(F32), im_of.astype(F32)
        for t in range(LAGS):
            c, s = cos_ref[t], sin_ref[t]
            out_ref[t, z, 0, w, :, lanes] = (re * c - im * s).astype(BF16)
            out_ref[t, z, 1, w, :, lanes] = (re * s + im * c).astype(BF16)

    for i in range(7):
        z = z_ref[i]

        def step(n, _, i=i, z=z):
            w, q = n // 4, n % 4
            lanes = pl.ds(pl.multiple_of(q * 128, 128), 128)
            turn(blocks[i][0, w, :, lanes], blocks[i][1, w, :, lanes], z, w, lanes)
            return _

        lax.fori_loop(0, 8, step, 0)
    z = z_ref[7]

    def last(n, _):
        w, q = n // 4, n % 4
        lanes = pl.ds(pl.multiple_of(q * 128, 128), 128)
        turn(blocks[7][w, :, lanes], blocks[8][w, :, lanes], z, w, lanes)
        return _

    lax.fori_loop(0, 8, last, 0)


def rotate(z_of, cosine, sine, blocks):
    _, w, f, n = blocks[0].shape
    out = pl.pallas_call(
        rotate_kernel,
        out_shape=jax.ShapeDtypeStruct((LAGS, ROWS, 2, w, f, n), BF16),
        in_specs=[SMEM] + [VMEM] * (2 + len(blocks)),
        out_specs=VMEM,
        cost_estimate=pl.CostEstimate(flops=20_000_000, bytes_accessed=8 << 20, transcendentals=0),
        compiler_params=pltpu.CompilerParams(vmem_limit_bytes=20 << 20),
        name="rotate",
    )(z_of, cosine, sine, *blocks)
    return out.reshape(LAGS, ROWS * 2 * w * f, n)


def gather_kernel(z_ref, *refs):
    out_ref = refs[-1]
    depth = refs[0].shape[1]
    for i, block in enumerate(refs[:-1]):
        out_ref[:, pl.ds(pl.multiple_of(z_ref[i] * depth, depth), depth)] = block[...]


def gather(z_of, blocks):
    n, depth = blocks[0].shape
    return pl.pallas_call(
        gather_kernel,
        out_shape=jax.ShapeDtypeStruct((n, depth * len(blocks)), BF16),
        in_specs=[SMEM] + [VMEM] * len(blocks),
        out_specs=VMEM,
        compiler_params=pltpu.CompilerParams(vmem_limit_bytes=8 << 20),
        name="gather",
    )(z_of, *blocks)


def product_kernel(scale, half_ref, rows_ref, turned_ref, *refs):
    out_ref = refs[-1]
    total = jnp.dot(rows_ref[...], turned_ref[0], preferred_element_type=F32)
    out_ref[0] = (total * scale).astype(BF16)


def product(half, rows, turned, scale, before=None):
    m, depth = rows.shape
    n = turned.shape[2]
    earlier = () if before is None else (before,)
    return pl.pallas_call(
        functools.partial(product_kernel, scale),
        out_shape=jax.ShapeDtypeStruct((LAGS, 2 * m, n), BF16),
        grid_spec=pltpu.PrefetchScalarGridSpec(
            num_scalar_prefetch=1,
            grid=(LAGS,),
            in_specs=[
                pl.BlockSpec((m, depth), lambda t, h: (0, 0)),
                pl.BlockSpec((1, depth, n), lambda t, h: (t, 0, 0)),
            ]
            + [pl.BlockSpec(memory_space=pl.ANY)] * len(earlier),
            out_specs=pl.BlockSpec((1, m, n), lambda t, h: (t, h[0], 0)),
        ),
        input_output_aliases={} if before is None else {3: 0},
        cost_estimate=pl.CostEstimate(flops=2 * LAGS * m * depth * n, bytes_accessed=10 << 20, transcendentals=0),
        compiler_params=pltpu.CompilerParams(vmem_limit_bytes=20 << 20),
        name="product",
    )(half, rows, turned, *earlier)


def phase_tables(bins, lags):
    freq = jnp.arange(bins).astype(F32) + 1.0
    shift = 2.0 * jnp.arange(lags).astype(F32) - lags + 1.0
    angle = math.pi * shift[:, None] * freq[None, :] / bins
    return jnp.cos(angle), jnp.sin(angle)


def body(spectra):
    row, col = lax.axis_index("row"), lax.axis_index("col")
    core = (col % 2).astype(jnp.int32)[None]
    bins = spectra.shape[2]
    white, white_t = whiten(spectra)

    sent = transpose_rows(white_t)
    down2, up2, down1, up1 = (along_z(white, s) for s in (2, -2, 1, -1))
    planes = [sent] + [in_plane(sent, *o) for o in PLANE]
    down3, up3 = along_z(down2, 1), along_z(up2, -1)
    far0, far1 = along_z(down2[0], 2), along_z(up2[1], -2)

    tables = [jnp.broadcast_to(t[:, :, None], (*t.shape, 128)) for t in phase_tables(bins, LAGS)]
    z_of = (row + jnp.array([0, -1, 1, -2, 2, -3, 3, 4], jnp.int32)) % ROWS
    turned = rotate(z_of, *tables, [white, down1, up1, down2, up2, down3, up3, far0, far1])

    slots = jnp.asarray(slot_table())[row, col // 2]
    rows = gather(slots, planes)
    others = other_core(rows)
    scale = 1.0 / math.sqrt(rows.shape[1] // 2)
    out = product(core, rows, turned, scale)
    return product(1 - core, others, turned, scale, out)


def solution(mesh):
    in_specs = (P(None, "row", "rep", "col"),)
    out_specs = P("rep", "row", "col")
    return jax.shard_map(body, mesh=mesh, in_specs=in_specs, out_specs=out_specs, check_vma=False)
```
